32 devices in a mesh: chan: 16 (over z, y, x), day: 2 (over core).
Axes of the slice: x: 2, y: 2, z: 4, core: 2. Of those that a mesh axis runs over, the one named last changes fastest.
Arguments:
- spectra: bfloat16 [512, 64, 400], P('chan', 'day'), may hold values from -6 to 6
- owners: int32 [2], replicated, may hold values from 0 to 15
Outputs:
- stacks: bfloat16 [2, 512, 32, 400], P(None, ('chan', 'day'))
The draws below stay inside these ranges and needn't reach their ends.
Inputs may be any that keep to these rules, and one draw needn't show every extreme that they name: `owners`: block indices along the channel axis; two steps may name the same block.
All inputs are finite; a program needn't handle non-finite values.
Results may differ from the reference program's by a relative error of at most 0.0073.
Values may be sent and summed in bfloat16 or wider, within the bound.
A program may use at most 64 MiB of HBM per device.

```python
import math
import jax
import jax.numpy as jnp
from jax import lax

F = 200
LAGS = 400
CH_DEV = 32
WIN_DEV = 32
STEPS = 2
CHANNELS = 512
WINDOWS = 64
N_CHAN = 16
N_DAY = 2


def block_scale(key, dims, split, smallest, largest):
    level = 1.0
    for axis_at, parts in split:
        steps = jax.random.uniform(jax.random.fold_in(jax.random.fold_in(key, 6), axis_at), (parts,), jnp.float32, smallest / len(split), largest / len(split))
        level = level * jnp.repeat(jnp.exp(steps), dims[axis_at] // parts).reshape((-1,) + (1,) * (len(dims) - 1 - axis_at))
    return level


def centred(own_key, extent, deviation, limit, cuts=(), held_as=jnp.bfloat16):
    result = deviation * jax.random.normal(own_key, extent, jnp.float32)
    if cuts:
        result = result * block_scale(own_key, extent, cuts, -0.22, 0.18)
    return jnp.clip(result, -limit, limit).astype(held_as)


def setup_inputs(seed: int = 0) -> dict:
    keys = jax.random.split(jax.random.key(seed), 3)
    return {
        "spectra": centred(keys[0], (CHANNELS, WINDOWS, 2 * F), 1.0, 6.0, ((0, 16), (1, 2))),
        "owners": jax.random.randint(keys[1], (STEPS,), 0, N_CHAN).astype(jnp.int32),
    }


def whiten(spectra, bins):
    values = spectra.astype(jnp.float32)
    real_part = values[..., :bins]
    imag_part = values[..., bins:]
    power = real_part * real_part + imag_part * imag_part
    mean_power = lax.optimization_barrier(jnp.mean(power, axis=-1, keepdims=True))
    factor = lax.rsqrt(power + 0.25 * mean_power + 1e-06)
    return jnp.concatenate([real_part * factor, imag_part * factor], axis=-1).astype(jnp.bfloat16)

def lag_table(bins, lag_count):
    freqs = jnp.arange(bins, dtype=jnp.int32)
    shifts = jnp.arange(lag_count, dtype=jnp.int32) - lag_count // 2
    phase = jnp.mod(freqs[:, None] * shifts[None, :], 2 * bins)
    angle = phase.astype(jnp.float32) * (math.pi / bins)
    return jnp.concatenate([jnp.cos(angle), -jnp.sin(angle)], axis=0).astype(jnp.bfloat16)

def day_cross(own, other, bins):
    own_f = own.astype(jnp.float32)
    other_f = other.astype(jnp.float32)
    own_re, own_im = (own_f[..., :bins], own_f[..., bins:])
    oth_re, oth_im = (other_f[..., :bins], other_f[..., bins:])
    cross_re = jnp.einsum('iwf,jwf->ijf', own_re, oth_re) + jnp.einsum('iwf,jwf->ijf', own_im, oth_im)
    cross_im = jnp.einsum('iwf,jwf->ijf', own_im, oth_re) - jnp.einsum('iwf,jwf->ijf', own_re, oth_im)
    return jnp.concatenate([cross_re, cross_im], axis=-1).astype(jnp.bfloat16)

def reference(spectra, owners):
    white = whiten(spectra, F)
    table = lag_table(F, LAGS)
    norm = 1.0 / math.sqrt(WINDOWS * F)
    groups = white.reshape(N_CHAN, CH_DEV, WINDOWS, 2 * F)
    results = []
    for step in range(STEPS):
        start = (owners[step] * CH_DEV).astype(jnp.int32)
        block = lax.dynamic_slice_in_dim(white, start, CH_DEV, 0)

        def one_group(own):
            total = jnp.zeros((CH_DEV, CH_DEV, 2 * F), jnp.float32)
            for day in range(N_DAY):
                lo = day * WIN_DEV
                part = day_cross(own[:, lo:lo + WIN_DEV], block[:, lo:lo + WIN_DEV], F)
                total = total + part.astype(jnp.float32)
            summed = total.astype(jnp.bfloat16).reshape(CH_DEV * CH_DEV, 2 * F)
            lagged = jnp.dot(summed, table, preferred_element_type=jnp.float32) * norm
            return lagged.reshape(CH_DEV, CH_DEV, LAGS).astype(jnp.bfloat16)
        stacked = lax.map(one_group, groups)
        results.append(stacked.reshape(CHANNELS, CH_DEV, LAGS))
    return jnp.stack(results, axis=0)
```

```python
import functools
import math

import jax
import jax.numpy as jnp
import numpy as np
from jax import lax
from jax.experimental import pallas as pl
from jax.experimental.pallas import tpu as pltpu
from jax.sharding import PartitionSpec as P

LAGS = 400
STEPS = 2
MESH_ID = pl.DeviceIdType.MESH


def whiten(spectra, bins):
    values = spectra.astype(jnp.float32)
    real_part = values[..., :bins]
    imag_part = values[..., bins:]
    power = real_part * real_part + imag_part * imag_part
    mean_power = jnp.mean(power, axis=-1, keepdims=True)
    factor = lax.rsqrt(power + 0.25 * mean_power + 1e-06)
    return (
        (real_part * factor).astype(jnp.bfloat16),
        (imag_part * factor).astype(jnp.bfloat16),
    )


def lag_table(bins, lag_count):
    freqs = np.arange(bins, dtype=np.int64)
    shifts = np.arange(lag_count, dtype=np.int64) - lag_count // 2
    phase = np.mod(freqs[:, None] * shifts[None, :], 2 * bins)
    angle = phase.astype(np.float32) * np.float32(math.pi / bins)
    return np.concatenate([np.cos(angle), -np.sin(angle)], axis=0).astype(jnp.bfloat16)


def chunks_of(piece):
    for count in (5, 4, 2):
        if piece % (count * 16) == 0:
            return count
    return 1


def kernel(
    line, chunks, chans, groups,
    owners_ref, a_ref, b_ref, o_ref,
    w_ref, r1_ref, s2_ref, r2_ref, zout_ref, zin_ref, c_send, c_recv,
    send_sem, recv_sem, day_send, day_recv,
):
    me = lax.axis_index("chan")
    day = lax.axis_index("day")
    cx = lax.rem(me, 2)
    cy = lax.rem(me // 2, 2)
    cz = me // 4
    nx = me + 1 - 2 * cx
    ny = me + 2 - 4 * cy
    rows = a_ref.shape[0]
    piece = rows // 4
    size = piece // chunks

    has_left = cz > 0
    has_right = cz < line - 1

    barrier = pltpu.get_barrier_semaphore()
    pl.semaphore_signal(barrier, inc=1, device_id={"chan": nx}, device_id_type=MESH_ID)
    pl.semaphore_signal(barrier, inc=1, device_id={"chan": ny}, device_id_type=MESH_ID)
    pl.semaphore_signal(barrier, inc=1, device_id={"day": 1 - day}, device_id_type=MESH_ID)

    @pl.when(has_left)
    def _():
        pl.semaphore_signal(barrier, inc=1, device_id={"chan": me - 4}, device_id_type=MESH_ID)

    @pl.when(has_right)
    def _():
        pl.semaphore_signal(barrier, inc=1, device_id={"chan": me + 4}, device_id_type=MESH_ID)

    inside = jnp.logical_and(has_left, has_right)

    @pl.when(inside)
    def _():
        pl.semaphore_wait(barrier, 5)

    @pl.when(jnp.logical_not(inside))
    def _():
        pl.semaphore_wait(barrier, 4 if line > 1 else 3)

    coords = ((cx, cy, nx, ny), (cy, cx, ny, nx))
    hits = []
    for step in range(STEPS):
        owner = owners_ref[step]
        ox = lax.rem(owner, 2)
        oy = lax.rem(owner // 2, 2)
        oz = owner // 4
        first = ox == cx if step == 0 else oy == cy
        second = oy == cy if step == 0 else ox == cx
        hits.append((first, second, oz == cz, oz < cz))

    def at(start, k):
        return pl.ds(pl.multiple_of(start + k * size, 16), size)

    def remote(src, dst, step, phase, k, chan):
        return pltpu.make_async_remote_copy(
            src_ref=src, dst_ref=dst,
            send_sem=send_sem.at[step, phase, k], recv_sem=recv_sem.at[step, phase, k],
            device_id={"chan": chan}, device_id_type=MESH_ID,
        )

    def scatter_first(step, part, k):
        ca, cb, na, nb = coords[step]
        pb = 1 - cb if part == 0 else cb
        return remote(
            a_ref.at[at((1 - ca) * 2 * piece + pb * piece, k)],
            r1_ref.at[step, part, pl.ds(k * size, size)], step, part, k, na,
        )

    def scatter_second(step, k):
        nb = coords[step][3]
        here = pl.ds(k * size, size)
        return remote(s2_ref.at[step, here], r2_ref.at[step, here], step, 2, k, nb)

    def along(step, k, up):
        here = pl.ds(k * size, size)
        side = 0 if up else 1
        return remote(
            zout_ref.at[side, step, here], zin_ref.at[side, step, here],
            step, 3 + side, k, me + 4 if up else me - 4,
        )

    def gather(step, k, phase):
        ca, cb, na, nb = coords[step]
        pb = 1 - cb if phase == 7 else cb
        where = at((ca * 2 + pb) * piece, k)
        return remote(
            w_ref.at[step, where], w_ref.at[step, where], step, phase, k, nb if phase == 5 else na
        )

    pairs = [(k, step) for k in range(chunks) for step in range(STEPS)]
    for part in range(2):
        for k, step in pairs:
            scatter_first(step, part, k).start()

    for k, step in pairs:
        ca, cb, _, _ = coords[step]
        scatter_first(step, 0, k).wait_recv()
        s2_ref[step, pl.ds(k * size, size)] = jnp.where(
            hits[step][0],
            a_ref[at(ca * 2 * piece + (1 - cb) * piece, k)],
            r1_ref[step, 0, pl.ds(k * size, size)],
        )
        scatter_second(step, k).start()

    for k, step in pairs:
        ca, cb, _, _ = coords[step]
        here = pl.ds(k * size, size)
        first, second, level, below = hits[step]
        scatter_first(step, 1, k).wait_recv()
        scatter_second(step, k).wait_recv()
        mine = jnp.where(
            second,
            jnp.where(first, a_ref[at((ca * 2 + cb) * piece, k)], r1_ref[step, 1, here]),
            r2_ref[step, here],
        )
        zout_ref[0, step, here] = mine
        zout_ref[1, step, here] = mine
        own = at((ca * 2 + cb) * piece, k)
        w_ref[step, own] = mine

        def upward():
            @pl.when(has_left)
            def _():
                along(step, k, True).wait_recv()
                got = zin_ref[0, step, here]
                zout_ref[0, step, here] = jnp.where(level, zout_ref[0, step, here], got)
                w_ref[step, own] = jnp.where(below, got, w_ref[step, own])

            @pl.when(has_right)
            def _():
                along(step, k, True).start()

        def downward():
            @pl.when(has_right)
            def _():
                along(step, k, False).wait_recv()
                got = zin_ref[1, step, here]
                zout_ref[1, step, here] = jnp.where(level, zout_ref[1, step, here], got)
                w_ref[step, own] = jnp.where(
                    level, w_ref[step, own], jnp.where(below, w_ref[step, own], got)
                )

            @pl.when(has_left)
            def _():
                along(step, k, False).start()

        @pl.when(cz < line // 2)
        def _():
            upward()
            downward()

        @pl.when(cz >= line // 2)
        def _():
            downward()
            upward()

        gather(step, k, 5).start()
        gather(step, k, 6).start()

    for k, step in pairs:
        gather(step, k, 5).wait_recv()
        gather(step, k, 7).start()

    for k, step in pairs:
        gather(step, k, 6).wait_recv()
        gather(step, k, 7).wait_recv()

    half = chans // 2
    keep = day * half
    give = (1 - day) * half
    lanes = lax.broadcasted_iota(jnp.int32, (chans, a_ref.shape[1]), 1)
    low = jnp.where(lanes < a_ref.shape[1] // 2, 1.0, 0.0).astype(jnp.bfloat16)
    high = jnp.where(lanes < a_ref.shape[1] // 2, 0.0, 1.0).astype(jnp.bfloat16)

    def cross(g, carry):
        base = pl.multiple_of(g * chans, 16)
        kept = pl.ds(pl.multiple_of(base + keep, 16), half)
        given = pl.ds(pl.multiple_of(base + give, 16), half)
        left = jnp.concatenate([a_ref[kept], b_ref[kept], a_ref[given], b_ref[given]], axis=0)
        blocks = []
        for step in range(STEPS):
            block = w_ref[step, pl.ds(base, chans)]
            blocks += [block * low, block * high]
        right = jnp.concatenate(blocks, axis=0)
        out = lax.dot_general(
            left, right, (((1,), (1,)), ((), ())), preferred_element_type=jnp.float32
        )
        spot = pl.ds(pl.multiple_of(g * chans, 16), chans)
        o_ref[spot] = out[:chans].astype(jnp.bfloat16)
        c_send[spot] = out[chans:].astype(jnp.bfloat16)
        return carry

    parts = day_send.shape[0]
    per = groups // parts

    def swap(part):
        where = pl.ds(part * per * chans, per * chans)
        return pltpu.make_async_remote_copy(
            src_ref=c_send.at[where], dst_ref=c_recv.at[where],
            send_sem=day_send.at[part], recv_sem=day_recv.at[part],
            device_id={"day": 1 - day}, device_id_type=MESH_ID,
        )

    for part in range(parts):
        lax.fori_loop(part * per, (part + 1) * per, cross, 0, unroll=5)
        swap(part).start()

    for part in range(parts):
        where = pl.ds(part * per * chans, per * chans)
        swap(part).wait_recv()
        total = o_ref[where].astype(jnp.float32) + c_recv[where].astype(jnp.float32)
        o_ref[where] = total.astype(jnp.bfloat16)

    for part in range(parts):
        swap(part).wait_send()
    for k, step in pairs:
        for part in range(2):
            scatter_first(step, part, k).wait_send()
        scatter_second(step, k).wait_send()
        for phase in (5, 6, 7):
            gather(step, k, phase).wait_send()

    @pl.when(has_right)
    def _():
        for k, step in pairs:
            along(step, k, True).wait_send()

    @pl.when(has_left)
    def _():
        for k, step in pairs:
            along(step, k, False).wait_send()


def local(spectra, owners):
    chans, windows, width = spectra.shape
    bins = width // 2
    groups = bins // 2
    line = lax.axis_size("chan") // 4
    windows_all = windows * lax.axis_size("day")
    re_part, im_part = whiten(spectra, bins)

    def packed(first, second):
        both = jnp.stack([first, second], axis=0).reshape(2, chans, windows, 2, groups)
        return both.transpose(4, 1, 3, 0, 2).reshape(groups * chans, 4 * windows)

    plain = packed(re_part, im_part)
    turned = packed(im_part, -re_part)
    rows, lanes = plain.shape
    piece = rows // 4
    chunks = chunks_of(piece)
    bf16 = jnp.bfloat16
    vmem = pl.BlockSpec(memory_space=pltpu.VMEM)
    summed = pl.pallas_call(
        functools.partial(kernel, line, chunks, chans, groups),
        out_shape=jax.ShapeDtypeStruct((groups * chans, 4 * chans), bf16),
        in_specs=[pl.BlockSpec(memory_space=pltpu.SMEM), vmem, vmem],
        out_specs=vmem,
        scratch_shapes=[
            pltpu.VMEM((STEPS, rows, lanes), bf16),
            pltpu.VMEM((STEPS, 2, piece, lanes), bf16),
            pltpu.VMEM((STEPS, piece, lanes), bf16),
            pltpu.VMEM((STEPS, piece, lanes), bf16),
            pltpu.VMEM((2, STEPS, piece, lanes), bf16),
            pltpu.VMEM((2, STEPS, piece, lanes), bf16),
            pltpu.VMEM((groups * chans, 4 * chans), bf16),
            pltpu.VMEM((groups * chans, 4 * chans), bf16),
            pltpu.SemaphoreType.DMA((STEPS, 8, chunks)),
            pltpu.SemaphoreType.DMA((STEPS, 8, chunks)),
            pltpu.SemaphoreType.DMA((4,)),
            pltpu.SemaphoreType.DMA((4,)),
        ],
        compiler_params=pltpu.CompilerParams(collective_id=0, has_side_effects=True),
    )(owners, plain, turned)

    norm = 1.0 / math.sqrt(windows_all * bins)
    table = jnp.asarray(lag_table(bins, LAGS)).reshape(2, 2, groups, LAGS)
    summed = summed.reshape(groups, 2, chans // 2, STEPS, 2, chans)
    lagged = jnp.einsum(
        "gcishj,chgl->sijl", summed, table, preferred_element_type=jnp.float32
    ) * norm
    return lagged.astype(bf16)


def solution(mesh):
    placed = (P("chan", "day", None), P())
    return jax.shard_map(
        local,
        mesh=mesh,
        in_specs=placed,
        out_specs=P(None, ("chan", "day"), None, None),
        check_vma=False,
    )
```

```python
import functools
import math

import jax
import jax.numpy as jnp
import numpy as np
from jax import lax
from jax.experimental import pallas as pl
from jax.experimental.pallas import tpu as pltpu
from jax.sharding import PartitionSpec as P

LAGS = 400
STEPS = 2
LAG = 4
MESH_ID = pl.DeviceIdType.MESH


def whiten(spectra, bins):
    values = spectra.astype(jnp.float32)
    real_part = values[..., :bins]
    imag_part = values[..., bins:]
    power = real_part * real_part + imag_part * imag_part
    mean_power = jnp.mean(power, axis=-1, keepdims=True)
    factor = lax.rsqrt(power + 0.25 * mean_power + 1e-06)
    return (
        (real_part * factor).astype(jnp.bfloat16),
        (imag_part * factor).astype(jnp.bfloat16),
    )


def lag_table(bins, lag_count):
    freqs = np.arange(bins, dtype=np.int64)
    shifts = np.arange(lag_count, dtype=np.int64) - lag_count // 2
    phase = np.mod(freqs[:, None] * shifts[None, :], 2 * bins)
    angle = phase.astype(np.float32) * np.float32(math.pi / bins)
    return np.concatenate([np.cos(angle), -np.sin(angle)], axis=0).astype(jnp.bfloat16)


def chunks_of(piece):
    for count in (5, 4, 2):
        if piece % (count * 16) == 0:
            return count
    return 1


def kernel(
    line, chunks, chans, groups,
    owners_ref, a_ref, o_ref,
    b_ref, w_ref, r1_ref, s2_ref, r2_ref, zout_ref, zin_ref, c_send, c_recv,
    send_sem, recv_sem, day_send, day_recv,
):
    me = lax.axis_index("chan")
    day = lax.axis_index("day")
    cx = lax.rem(me, 2)
    cy = lax.rem(me // 2, 2)
    cz = me // 4
    nx = me + 1 - 2 * cx
    ny = me + 2 - 4 * cy
    rows = a_ref.shape[0]
    piece = rows // 4
    size = piece // chunks

    has_left = cz > 0
    has_right = cz < line - 1

    barrier = pltpu.get_barrier_semaphore()
    pl.semaphore_signal(barrier, inc=1, device_id={"chan": nx}, device_id_type=MESH_ID)
    pl.semaphore_signal(barrier, inc=1, device_id={"chan": ny}, device_id_type=MESH_ID)
    pl.semaphore_signal(barrier, inc=1, device_id={"day": 1 - day}, device_id_type=MESH_ID)

    @pl.when(has_left)
    def _():
        pl.semaphore_signal(barrier, inc=1, device_id={"chan": me - 4}, device_id_type=MESH_ID)

    @pl.when(has_right)
    def _():
        pl.semaphore_signal(barrier, inc=1, device_id={"chan": me + 4}, device_id_type=MESH_ID)

    inside = jnp.logical_and(has_left, has_right)

    @pl.when(inside)
    def _():
        pl.semaphore_wait(barrier, 5)

    @pl.when(jnp.logical_not(inside))
    def _():
        pl.semaphore_wait(barrier, 4 if line > 1 else 3)

    coords = ((cx, cy, nx, ny), (cy, cx, ny, nx))
    hits = []
    for step in range(STEPS):
        owner = owners_ref[step]
        ox = lax.rem(owner, 2)
        oy = lax.rem(owner // 2, 2)
        oz = owner // 4
        first = ox == cx if step == 0 else oy == cy
        second = oy == cy if step == 0 else ox == cx
        hits.append((first, second, oz == cz, oz < cz))

    def at(start, k):
        return pl.ds(pl.multiple_of(start + k * size, 16), size)

    def remote(src, dst, step, phase, k, chan):
        return pltpu.make_async_remote_copy(
            src_ref=src, dst_ref=dst,
            send_sem=send_sem.at[step, phase, k], recv_sem=recv_sem.at[step, phase, k],
            device_id={"chan": chan}, device_id_type=MESH_ID,
        )

    def scatter_first(step, part, k):
        ca, cb, na, nb = coords[step]
        pb = 1 - cb if part == 0 else cb
        return remote(
            a_ref.at[at((1 - ca) * 2 * piece + pb * piece, k)],
            r1_ref.at[step, part, pl.ds(k * size, size)], step, part, k, na,
        )

    def scatter_second(step, k):
        nb = coords[step][3]
        here = pl.ds(k * size, size)
        return remote(s2_ref.at[step, here], r2_ref.at[step, here], step, 2, k, nb)

    def along(step, k, up):
        here = pl.ds(k * size, size)
        side = 0 if up else 1
        return remote(
            zout_ref.at[side, step, here], zin_ref.at[side, step, here],
            step, 3 + side, k, me + 4 if up else me - 4,
        )

    def gather(step, k, phase):
        ca, cb, na, nb = coords[step]
        pb = 1 - cb if phase == 7 else cb
        where = at((ca * 2 + pb) * piece, k)
        return remote(
            w_ref.at[step, where], w_ref.at[step, where], step, phase, k, nb if phase == 5 else na
        )

    pairs = [(k, step) for k in range(chunks) for step in range(STEPS)]
    for part in range(2):
        for k, step in pairs:
            scatter_first(step, part, k).start()

    lanes_all = a_ref.shape[1]
    quarter = lanes_all // 4
    from_lane = lax.broadcasted_iota(jnp.int32, (lanes_all, lanes_all), 0)
    to_lane = lax.broadcasted_iota(jnp.int32, (lanes_all, lanes_all), 1)
    is_re = lax.rem(to_lane // quarter, 2) == 0
    turn = jnp.where(
        is_re,
        jnp.where(from_lane == to_lane + quarter, 1.0, 0.0),
        jnp.where(from_lane + quarter == to_lane, -1.0, 0.0),
    ).astype(jnp.bfloat16)
    block_rows = rows // 5 if rows % 80 == 0 else rows

    def turn_rows(i, carry):
        some = pl.ds(pl.multiple_of(i * block_rows, 16), block_rows)
        b_ref[some] = jnp.dot(
            a_ref[some], turn, preferred_element_type=jnp.float32
        ).astype(jnp.bfloat16)
        return carry

    lax.fori_loop(0, rows // block_rows, turn_rows, 0)

    for k, step in pairs:
        ca, cb, _, _ = coords[step]
        scatter_first(step, 0, k).wait_recv()
        s2_ref[step, pl.ds(k * size, size)] = jnp.where(
            hits[step][0],
            a_ref[at(ca * 2 * piece + (1 - cb) * piece, k)],
            r1_ref[step, 0, pl.ds(k * size, size)],
        )
        scatter_second(step, k).start()

    def ready(k, step):
        ca, cb, _, _ = coords[step]
        here = pl.ds(k * size, size)
        first, second, _, _ = hits[step]
        scatter_first(step, 1, k).wait_recv()
        scatter_second(step, k).wait_recv()
        mine = jnp.where(
            second,
            jnp.where(first, a_ref[at((ca * 2 + cb) * piece, k)], r1_ref[step, 1, here]),
            r2_ref[step, here],
        )
        zout_ref[0, step, here] = mine
        zout_ref[1, step, here] = mine
        own = at((ca * 2 + cb) * piece, k)
        w_ref[step, own] = mine

    def stream(k, step, up):
        ca, cb, _, _ = coords[step]
        here = pl.ds(k * size, size)
        own = at((ca * 2 + cb) * piece, k)
        _, _, level, below = hits[step]
        side = 0 if up else 1
        source = below if up else jnp.logical_not(jnp.logical_or(level, below))

        @pl.when(has_left if up else has_right)
        def _():
            along(step, k, up).wait_recv()
            got = zin_ref[side, step, here]
            zout_ref[side, step, here] = jnp.where(level, zout_ref[side, step, here], got)
            w_ref[step, own] = jnp.where(source, got, w_ref[step, own])

        @pl.when(has_right if up else has_left)
        def _():
            along(step, k, up).start()

    def both_ways(near, far):
        @pl.when(cz < line // 2)
        def _():
            if near is not None:
                stream(*near, True)
            if far is not None:
                stream(*far, False)

        @pl.when(cz >= line // 2)
        def _():
            if near is not None:
                stream(*near, False)
            if far is not None:
                stream(*far, True)

    count = len(pairs)
    for tick in range(count + LAG):
        near = far = None
        if tick < count:
            near = pairs[tick]
            ready(*near)
        if tick >= LAG:
            far = pairs[tick - LAG]
        both_ways(near, far)
        if far is not None:
            gather(far[1], far[0], 5).start()
            gather(far[1], far[0], 6).start()

    for k, step in pairs:
        gather(step, k, 5).wait_recv()
        gather(step, k, 7).start()

    for k, step in pairs:
        gather(step, k, 6).wait_recv()
        gather(step, k, 7).wait_recv()

    half = chans // 2
    keep = day * half
    give = (1 - day) * half
    lanes = lax.broadcasted_iota(jnp.int32, (chans, a_ref.shape[1]), 1)
    low = jnp.where(lanes < a_ref.shape[1] // 2, 1.0, 0.0).astype(jnp.bfloat16)
    high = jnp.where(lanes < a_ref.shape[1] // 2, 0.0, 1.0).astype(jnp.bfloat16)

    def cross(g, carry):
        base = pl.multiple_of(g * chans, 16)
        kept = pl.ds(pl.multiple_of(base + keep, 16), half)
        given = pl.ds(pl.multiple_of(base + give, 16), half)
        left = jnp.concatenate([a_ref[kept], b_ref[kept], a_ref[given], b_ref[given]], axis=0)
        blocks = []
        for step in range(STEPS):
            block = w_ref[step, pl.ds(base, chans)]
            blocks += [block * low, block * high]
        right = jnp.concatenate(blocks, axis=0)
        out = lax.dot_general(
            left, right, (((1,), (1,)), ((), ())), preferred_element_type=jnp.float32
        )
        spot = pl.ds(pl.multiple_of(g * chans, 16), chans)
        o_ref[spot] = out[:chans].astype(jnp.bfloat16)
        c_send[spot] = out[chans:].astype(jnp.bfloat16)
        return carry

    parts = day_send.shape[0]
    per = groups // parts

    def swap(part):
        where = pl.ds(part * per * chans, per * chans)
        return pltpu.make_async_remote_copy(
            src_ref=c_send.at[where], dst_ref=c_recv.at[where],
            send_sem=day_send.at[part], recv_sem=day_recv.at[part],
            device_id={"day": 1 - day}, device_id_type=MESH_ID,
        )

    for part in range(parts):
        lax.fori_loop(part * per, (part + 1) * per, cross, 0, unroll=5)
        swap(part).start()

    for part in range(parts):
        where = pl.ds(part * per * chans, per * chans)
        swap(part).wait_recv()
        total = o_ref[where].astype(jnp.float32) + c_recv[where].astype(jnp.float32)
        o_ref[where] = total.astype(jnp.bfloat16)

    for part in range(parts):
        swap(part).wait_send()
    for k, step in pairs:
        for part in range(2):
            scatter_first(step, part, k).wait_send()
        scatter_second(step, k).wait_send()
        for phase in (5, 6, 7):
            gather(step, k, phase).wait_send()

    @pl.when(has_right)
    def _():
        for k, step in pairs:
            along(step, k, True).wait_send()

    @pl.when(has_left)
    def _():
        for k, step in pairs:
            along(step, k, False).wait_send()


def local(spectra, owners):
    chans, windows, width = spectra.shape
    bins = width // 2
    groups = bins // 2
    line = lax.axis_size("chan") // 4
    windows_all = windows * lax.axis_size("day")
    re_part, im_part = whiten(spectra, bins)

    plain = jnp.concatenate(
        [re_part[..., :groups], im_part[..., :groups], re_part[..., groups:], im_part[..., groups:]],
        axis=1,
    )
    plain = lax.optimization_barrier(plain)
    plain = plain.transpose(2, 0, 1).reshape(groups * chans, 4 * windows)
    rows, lanes = plain.shape
    piece = rows // 4
    chunks = chunks_of(piece)
    bf16 = jnp.bfloat16
    vmem = pl.BlockSpec(memory_space=pltpu.VMEM)
    summed = pl.pallas_call(
        functools.partial(kernel, line, chunks, chans, groups),
        out_shape=jax.ShapeDtypeStruct((groups * chans, 4 * chans), bf16),
        in_specs=[pl.BlockSpec(memory_space=pltpu.SMEM), vmem],
        out_specs=vmem,
        scratch_shapes=[
            pltpu.VMEM((rows, lanes), bf16),
            pltpu.VMEM((STEPS, rows, lanes), bf16),
            pltpu.VMEM((STEPS, 2, piece, lanes), bf16),
            pltpu.VMEM((STEPS, piece, lanes), bf16),
            pltpu.VMEM((STEPS, piece, lanes), bf16),
            pltpu.VMEM((2, STEPS, piece, lanes), bf16),
            pltpu.VMEM((2, STEPS, piece, lanes), bf16),
            pltpu.VMEM((groups * chans, 4 * chans), bf16),
            pltpu.VMEM((groups * chans, 4 * chans), bf16),
            pltpu.SemaphoreType.DMA((STEPS, 8, chunks)),
            pltpu.SemaphoreType.DMA((STEPS, 8, chunks)),
            pltpu.SemaphoreType.DMA((4,)),
            pltpu.SemaphoreType.DMA((4,)),
        ],
        compiler_params=pltpu.CompilerParams(collective_id=0, has_side_effects=True),
    )(owners, plain)

    norm = 1.0 / math.sqrt(windows_all * bins)
    table = jnp.asarray(lag_table(bins, LAGS))
    half = chans // 2
    turned = summed.reshape(groups, chans, 4 * chans).transpose(1, 2, 0)
    turned = lax.optimization_barrier(turned).reshape(2, half, STEPS, 2, chans, groups)
    full = jnp.concatenate(
        [turned[part, :, :, which] for part in range(2) for which in range(2)], axis=-1
    )
    full = full.transpose(1, 0, 2, 3).reshape(STEPS * half * chans, 2 * bins)
    lagged = jnp.dot(full, table, preferred_element_type=jnp.float32) * norm
    lagged = lagged.reshape(STEPS, half, chans, LAGS)
    return lagged.astype(bf16)


def solution(mesh):
    placed = (P("chan", "day", None), P())
    return jax.shard_map(
        local,
        mesh=mesh,
        in_specs=placed,
        out_specs=P(None, ("chan", "day"), None, None),
        check_vma=False,
    )
```

```python
import functools
import math

import jax
import jax.numpy as jnp
import numpy as np
from jax import lax
from jax.experimental import pallas as pl
from jax.experimental.pallas import tpu as pltpu
from jax.sharding import PartitionSpec as P

LAGS = 400
STEPS = 2
LAG = 10
MESH_ID = pl.DeviceIdType.MESH


def whiten(spectra, bins):
    values = spectra.astype(jnp.float32)
    real_part = values[..., :bins]
    imag_part = values[..., bins:]
    power = real_part * real_part + imag_part * imag_part
    mean_power = jnp.mean(power, axis=-1, keepdims=True)
    factor = lax.rsqrt(power + 0.25 * mean_power + 1e-06)
    return (
        (real_part * factor).astype(jnp.bfloat16),
        (imag_part * factor).astype(jnp.bfloat16),
    )


def lag_table(bins, lag_count):
    freqs = np.arange(bins, dtype=np.int64)
    shifts = np.arange(lag_count, dtype=np.int64) - lag_count // 2
    phase = np.mod(freqs[:, None] * shifts[None, :], 2 * bins)
    angle = phase.astype(np.float32) * np.float32(math.pi / bins)
    return np.concatenate([np.cos(angle), -np.sin(angle)], axis=0).astype(jnp.bfloat16)


def chunks_of(piece):
    for count in (5, 4, 2):
        if piece % (count * 16) == 0:
            return count
    return 1


def kernel(
    line, chunks, chans, groups,
    owners_ref, a_ref, o_ref,
    b_ref, w_ref, r1_ref, s2_ref, r2_ref, zout_ref, zin_ref, c_send, c_recv,
    send_sem, recv_sem, day_send, day_recv,
):
    me = lax.axis_index("chan")
    day = lax.axis_index("day")
    cx = lax.rem(me, 2)
    cy = lax.rem(me // 2, 2)
    cz = me // 4
    nx = me + 1 - 2 * cx
    ny = me + 2 - 4 * cy
    rows = a_ref.shape[0]
    piece = rows // 4
    size = piece // chunks

    has_left = cz > 0
    has_right = cz < line - 1

    barrier = pltpu.get_barrier_semaphore()
    pl.semaphore_signal(barrier, inc=1, device_id={"chan": nx}, device_id_type=MESH_ID)
    pl.semaphore_signal(barrier, inc=1, device_id={"chan": ny}, device_id_type=MESH_ID)
    pl.semaphore_signal(barrier, inc=1, device_id={"day": 1 - day}, device_id_type=MESH_ID)

    @pl.when(has_left)
    def _():
        pl.semaphore_signal(barrier, inc=1, device_id={"chan": me - 4}, device_id_type=MESH_ID)

    @pl.when(has_right)
    def _():
        pl.semaphore_signal(barrier, inc=1, device_id={"chan": me + 4}, device_id_type=MESH_ID)

    inside = jnp.logical_and(has_left, has_right)

    @pl.when(inside)
    def _():
        pl.semaphore_wait(barrier, 5)

    @pl.when(jnp.logical_not(inside))
    def _():
        pl.semaphore_wait(barrier, 4 if line > 1 else 3)

    coords = ((cx, cy, nx, ny), (cy, cx, ny, nx))
    hits = []
    for step in range(STEPS):
        owner = owners_ref[step]
        ox = lax.rem(owner, 2)
        oy = lax.rem(owner // 2, 2)
        oz = owner // 4
        first = ox == cx if step == 0 else oy == cy
        second = oy == cy if step == 0 else ox == cx
        hits.append((first, second, oz == cz, oz < cz))

    def at(start, k):
        return pl.ds(pl.multiple_of(start + k * size, 16), size)

    def remote(src, dst, step, phase, k, chan):
        return pltpu.make_async_remote_copy(
            src_ref=src, dst_ref=dst,
            send_sem=send_sem.at[step, phase, k], recv_sem=recv_sem.at[step, phase, k],
            device_id={"chan": chan}, device_id_type=MESH_ID,
        )

    def scatter_first(step, part, k):
        ca, cb, na, nb = coords[step]
        pb = 1 - cb if part == 0 else cb
        return remote(
            a_ref.at[at((1 - ca) * 2 * piece + pb * piece, k)],
            r1_ref.at[step, part, pl.ds(k * size, size)], step, part, k, na,
        )

    def scatter_second(step, k):
        nb = coords[step][3]
        here = pl.ds(k * size, size)
        return remote(s2_ref.at[step, here], r2_ref.at[step, here], step, 2, k, nb)

    def along(step, k, up):
        here = pl.ds(k * size, size)
        side = 0 if up else 1
        return remote(
            zout_ref.at[side, step, here], zin_ref.at[side, step, here],
            step, 3 + side, k, me + 4 if up else me - 4,
        )

    def gather(step, k, phase):
        ca, cb, na, nb = coords[step]
        pb = 1 - cb if phase == 7 else cb
        where = at((ca * 2 + pb) * piece, k)
        return remote(
            w_ref.at[step, where], w_ref.at[step, where], step, phase, k, nb if phase == 5 else na
        )

    pairs = [(k, step) for k in range(chunks) for step in range(STEPS)]
    for part in range(2):
        for k, step in pairs:
            scatter_first(step, part, k).start()

    lanes_all = a_ref.shape[1]
    quarter = lanes_all // 4
    from_lane = lax.broadcasted_iota(jnp.int32, (lanes_all, lanes_all), 0)
    to_lane = lax.broadcasted_iota(jnp.int32, (lanes_all, lanes_all), 1)
    is_re = lax.rem(to_lane // quarter, 2) == 0
    turn = jnp.where(
        is_re,
        jnp.where(from_lane == to_lane + quarter, 1.0, 0.0),
        jnp.where(from_lane + quarter == to_lane, -1.0, 0.0),
    ).astype(jnp.bfloat16)
    block_rows = rows // 5 if rows % 80 == 0 else rows

    def turn_rows(i, carry):
        some = pl.ds(pl.multiple_of(i * block_rows, 16), block_rows)
        b_ref[some] = jnp.dot(
            a_ref[some], turn, preferred_element_type=jnp.float32
        ).astype(jnp.bfloat16)
        return carry

    lax.fori_loop(0, rows // block_rows, turn_rows, 0)

    for k, step in pairs:
        ca, cb, _, _ = coords[step]
        scatter_first(step, 0, k).wait_recv()
        s2_ref[step, pl.ds(k * size, size)] = jnp.where(
            hits[step][0],
            a_ref[at(ca * 2 * piece + (1 - cb) * piece, k)],
            r1_ref[step, 0, pl.ds(k * size, size)],
        )
        scatter_second(step, k).start()

    def ready(k, step):
        ca, cb, _, _ = coords[step]
        here = pl.ds(k * size, size)
        first, second, _, _ = hits[step]
        scatter_first(step, 1, k).wait_recv()
        scatter_second(step, k).wait_recv()
        mine = jnp.where(
            second,
            jnp.where(first, a_ref[at((ca * 2 + cb) * piece, k)], r1_ref[step, 1, here]),
            r2_ref[step, here],
        )
        zout_ref[0, step, here] = mine
        zout_ref[1, step, here] = mine
        own = at((ca * 2 + cb) * piece, k)
        w_ref[step, own] = mine

    def stream(k, step, up):
        ca, cb, _, _ = coords[step]
        here = pl.ds(k * size, size)
        own = at((ca * 2 + cb) * piece, k)
        _, _, level, below = hits[step]
        side = 0 if up else 1
        source = below if up else jnp.logical_not(jnp.logical_or(level, below))

        @pl.when(has_left if up else has_right)
        def _():
            along(step, k, up).wait_recv()
            got = zin_ref[side, step, here]
            zout_ref[side, step, here] = jnp.where(level, zout_ref[side, step, here], got)
            w_ref[step, own] = jnp.where(source, got, w_ref[step, own])

        @pl.when(has_right if up else has_left)
        def _():
            along(step, k, up).start()

    def both_ways(near, far):
        @pl.when(cz < line // 2)
        def _():
            if near is not None:
                stream(*near, True)
            if far is not None:
                stream(*far, False)

        @pl.when(cz >= line // 2)
        def _():
            if near is not None:
                stream(*near, False)
            if far is not None:
                stream(*far, True)

    count = len(pairs)
    for tick in range(count + LAG):
        near = far = None
        if tick < count:
            near = pairs[tick]
            ready(*near)
        if tick >= LAG:
            far = pairs[tick - LAG]
        both_ways(near, far)
        if far is not None:
            gather(far[1], far[0], 5).start()
            gather(far[1], far[0], 6).start()

    for k, step in pairs:
        gather(step, k, 5).wait_recv()
        gather(step, k, 7).start()

    for k, step in pairs:
        gather(step, k, 6).wait_recv()
        gather(step, k, 7).wait_recv()

    half = chans // 2
    keep = day * half
    give = (1 - day) * half
    lanes = lax.broadcasted_iota(jnp.int32, (chans, a_ref.shape[1]), 1)
    low = jnp.where(lanes < a_ref.shape[1] // 2, 1.0, 0.0).astype(jnp.bfloat16)
    high = jnp.where(lanes < a_ref.shape[1] // 2, 0.0, 1.0).astype(jnp.bfloat16)

    def cross(g, carry):
        base = pl.multiple_of(g * chans, 16)
        kept = pl.ds(pl.multiple_of(base + keep, 16), half)
        given = pl.ds(pl.multiple_of(base + give, 16), half)
        left = jnp.concatenate([a_ref[kept], b_ref[kept], a_ref[given], b_ref[given]], axis=0)
        blocks = []
        for step in range(STEPS):
            block = w_ref[step, pl.ds(base, chans)]
            blocks += [block * low, block * high]
        right = jnp.concatenate(blocks, axis=0)
        out = lax.dot_general(
            left, right, (((1,), (1,)), ((), ())), preferred_element_type=jnp.float32
        )
        spot = pl.ds(pl.multiple_of(g * chans, 16), chans)
        o_ref[spot] = out[:chans].astype(jnp.bfloat16)
        c_send[spot] = out[chans:].astype(jnp.bfloat16)
        return carry

    parts = day_send.shape[0]
    per = groups // parts

    def swap(part):
        where = pl.ds(part * per * chans, per * chans)
        return pltpu.make_async_remote_copy(
            src_ref=c_send.at[where], dst_ref=c_recv.at[where],
            send_sem=day_send.at[part], recv_sem=day_recv.at[part],
            device_id={"day": 1 - day}, device_id_type=MESH_ID,
        )

    for part in range(parts):
        lax.fori_loop(part * per, (part + 1) * per, cross, 0, unroll=5)
        swap(part).start()

    for part in range(parts):
        where = pl.ds(part * per * chans, per * chans)
        swap(part).wait_recv()
        total = o_ref[where].astype(jnp.float32) + c_recv[where].astype(jnp.float32)
        o_ref[where] = total.astype(jnp.bfloat16)

    for part in range(parts):
        swap(part).wait_send()
    for k, step in pairs:
        for part in range(2):
            scatter_first(step, part, k).wait_send()
        scatter_second(step, k).wait_send()
        for phase in (5, 6, 7):
            gather(step, k, phase).wait_send()

    @pl.when(has_right)
    def _():
        for k, step in pairs:
            along(step, k, True).wait_send()

    @pl.when(has_left)
    def _():
        for k, step in pairs:
            along(step, k, False).wait_send()


def local(spectra, owners):
    chans, windows, width = spectra.shape
    bins = width // 2
    groups = bins // 2
    line = lax.axis_size("chan") // 4
    windows_all = windows * lax.axis_size("day")
    re_part, im_part = whiten(spectra, bins)

    plain = jnp.concatenate(
        [re_part[..., :groups], im_part[..., :groups], re_part[..., groups:], im_part[..., groups:]],
        axis=1,
    )
    plain = lax.optimization_barrier(plain)
    plain = plain.transpose(2, 0, 1).reshape(groups * chans, 4 * windows)
    rows, lanes = plain.shape
    piece = rows // 4
    chunks = chunks_of(piece)
    bf16 = jnp.bfloat16
    vmem = pl.BlockSpec(memory_space=pltpu.VMEM)
    summed = pl.pallas_call(
        functools.partial(kernel, line, chunks, chans, groups),
        out_shape=jax.ShapeDtypeStruct((groups * chans, 4 * chans), bf16),
        in_specs=[pl.BlockSpec(memory_space=pltpu.SMEM), vmem],
        out_specs=vmem,
        scratch_shapes=[
            pltpu.VMEM((rows, lanes), bf16),
            pltpu.VMEM((STEPS, rows, lanes), bf16),
            pltpu.VMEM((STEPS, 2, piece, lanes), bf16),
            pltpu.VMEM((STEPS, piece, lanes), bf16),
            pltpu.VMEM((STEPS, piece, lanes), bf16),
            pltpu.VMEM((2, STEPS, piece, lanes), bf16),
            pltpu.VMEM((2, STEPS, piece, lanes), bf16),
            pltpu.VMEM((groups * chans, 4 * chans), bf16),
            pltpu.VMEM((groups * chans, 4 * chans), bf16),
            pltpu.SemaphoreType.DMA((STEPS, 8, chunks)),
            pltpu.SemaphoreType.DMA((STEPS, 8, chunks)),
            pltpu.SemaphoreType.DMA((4,)),
            pltpu.SemaphoreType.DMA((4,)),
        ],
        compiler_params=pltpu.CompilerParams(collective_id=0, has_side_effects=True),
    )(owners, plain)

    norm = 1.0 / math.sqrt(windows_all * bins)
    table = jnp.asarray(lag_table(bins, LAGS))
    half = chans // 2
    turned = summed.reshape(groups, chans, 4 * chans).transpose(1, 2, 0)
    turned = lax.optimization_barrier(turned).reshape(2, half, STEPS, 2, chans, groups)
    full = jnp.concatenate(
        [turned[part, :, :, which] for part in range(2) for which in range(2)], axis=-1
    )
    full = full.transpose(1, 0, 2, 3).reshape(STEPS * half * chans, 2 * bins)
    lagged = jnp.dot(full, table, preferred_element_type=jnp.float32) * norm
    lagged = lagged.reshape(STEPS, half, chans, LAGS)
    return lagged.astype(bf16)


def solution(mesh):
    placed = (P("chan", "day", None), P())
    return jax.shard_map(
        local,
        mesh=mesh,
        in_specs=placed,
        out_specs=P(None, ("chan", "day"), None, None),
        check_vma=False,
    )
```

```python
import functools
import math

import jax
import jax.numpy as jnp
import numpy as np
from jax import lax
from jax.experimental import pallas as pl
from jax.experimental.pallas import tpu as pltpu
from jax.sharding import PartitionSpec as P

LAGS = 400
STEPS = 2
LAG = 10
MESH_ID = pl.DeviceIdType.MESH


def whiten(spectra, bins):
    values = spectra.astype(jnp.float32)
    real_part = values[..., :bins]
    imag_part = values[..., bins:]
    power = real_part * real_part + imag_part * imag_part
    mean_power = jnp.mean(power, axis=-1, keepdims=True)
    factor = lax.rsqrt(power + 0.25 * mean_power + 1e-06)
    return (
        (real_part * factor).astype(jnp.bfloat16),
        (imag_part * factor).astype(jnp.bfloat16),
    )


def lag_table(bins, lag_count):
    freqs = np.arange(bins, dtype=np.int64)
    shifts = np.arange(lag_count, dtype=np.int64) - lag_count // 2
    phase = np.mod(freqs[:, None] * shifts[None, :], 2 * bins)
    angle = phase.astype(np.float32) * np.float32(math.pi / bins)
    return np.concatenate([np.cos(angle), -np.sin(angle)], axis=0).astype(jnp.bfloat16)


def chunks_of(piece):
    for count in (5, 4, 2):
        if piece % (count * 16) == 0:
            return count
    return 1


def kernel(
    line, chunks, chans, groups,
    owners_ref, a_ref, o_ref,
    b_ref, w_ref, r1_ref, s2_ref, r2_ref, zout_ref, zin_ref, c_send, c_recv,
    send_sem, recv_sem, day_send, day_recv,
):
    me = lax.axis_index("chan")
    day = lax.axis_index("day")
    cx = lax.rem(me, 2)
    cy = lax.rem(me // 2, 2)
    cz = me // 4
    nx = me + 1 - 2 * cx
    ny = me + 2 - 4 * cy
    rows = a_ref.shape[0]
    piece = rows // 4
    size = piece // chunks

    has_left = cz > 0
    has_right = cz < line - 1

    barrier = pltpu.get_barrier_semaphore()
    pl.semaphore_signal(barrier, inc=1, device_id={"chan": nx}, device_id_type=MESH_ID)
    pl.semaphore_signal(barrier, inc=1, device_id={"chan": ny}, device_id_type=MESH_ID)
    pl.semaphore_signal(barrier, inc=1, device_id={"day": 1 - day}, device_id_type=MESH_ID)

    @pl.when(has_left)
    def _():
        pl.semaphore_signal(barrier, inc=1, device_id={"chan": me - 4}, device_id_type=MESH_ID)

    @pl.when(has_right)
    def _():
        pl.semaphore_signal(barrier, inc=1, device_id={"chan": me + 4}, device_id_type=MESH_ID)

    inside = jnp.logical_and(has_left, has_right)

    @pl.when(inside)
    def _():
        pl.semaphore_wait(barrier, 5)

    @pl.when(jnp.logical_not(inside))
    def _():
        pl.semaphore_wait(barrier, 4 if line > 1 else 3)

    coords = ((cx, cy, nx, ny), (cy, cx, ny, nx))
    hits = []
    for step in range(STEPS):
        owner = owners_ref[step]
        ox = lax.rem(owner, 2)
        oy = lax.rem(owner // 2, 2)
        oz = owner // 4
        first = ox == cx if step == 0 else oy == cy
        second = oy == cy if step == 0 else ox == cx
        hits.append((first, second, oz == cz, oz < cz))

    def at(start, k):
        return pl.ds(pl.multiple_of(start + k * size, 16), size)

    def remote(src, dst, step, phase, k, chan):
        return pltpu.make_async_remote_copy(
            src_ref=src, dst_ref=dst,
            send_sem=send_sem.at[step, phase, k], recv_sem=recv_sem.at[step, phase, k],
            device_id={"chan": chan}, device_id_type=MESH_ID,
        )

    def scatter_first(step, part, k):
        ca, cb, na, nb = coords[step]
        pb = 1 - cb if part == 0 else cb
        return remote(
            a_ref.at[at((1 - ca) * 2 * piece + pb * piece, k)],
            r1_ref.at[step, part, pl.ds(k * size, size)], step, part, k, na,
        )

    def scatter_second(step, k):
        nb = coords[step][3]
        here = pl.ds(k * size, size)
        return remote(s2_ref.at[step, here], r2_ref.at[step, here], step, 2, k, nb)

    def along(step, k, up):
        here = pl.ds(k * size, size)
        side = 0 if up else 1
        return remote(
            zout_ref.at[side, step, here], zin_ref.at[side, step, here],
            step, 3 + side, k, me + 4 if up else me - 4,
        )

    def gather(step, k, phase):
        ca, cb, na, nb = coords[step]
        pb = 1 - cb if phase == 7 else cb
        where = at((ca * 2 + pb) * piece, k)
        return remote(
            w_ref.at[step, where], w_ref.at[step, where], step, phase, k, nb if phase == 5 else na
        )

    pairs = [(k, step) for k in range(chunks) for step in range(STEPS)]
    for part in range(2):
        for k, step in pairs:
            scatter_first(step, part, k).start()

    lanes_all = a_ref.shape[1]
    quarter = lanes_all // 4
    from_lane = lax.broadcasted_iota(jnp.int32, (lanes_all, lanes_all), 0)
    to_lane = lax.broadcasted_iota(jnp.int32, (lanes_all, lanes_all), 1)
    is_re = lax.rem(to_lane // quarter, 2) == 0
    turn = jnp.where(
        is_re,
        jnp.where(from_lane == to_lane + quarter, 1.0, 0.0),
        jnp.where(from_lane + quarter == to_lane, -1.0, 0.0),
    ).astype(jnp.bfloat16)
    block_rows = rows // 5 if rows % 80 == 0 else rows

    def turn_rows(i, carry):
        some = pl.ds(pl.multiple_of(i * block_rows, 16), block_rows)
        b_ref[some] = jnp.dot(
            a_ref[some], turn, preferred_element_type=jnp.float32
        ).astype(jnp.bfloat16)
        return carry

    lax.fori_loop(0, rows // block_rows, turn_rows, 0)

    for k, step in pairs:
        ca, cb, _, _ = coords[step]
        scatter_first(step, 0, k).wait_recv()
        s2_ref[step, pl.ds(k * size, size)] = jnp.where(
            hits[step][0],
            a_ref[at(ca * 2 * piece + (1 - cb) * piece, k)],
            r1_ref[step, 0, pl.ds(k * size, size)],
        )
        scatter_second(step, k).start()

    def ready(k, step):
        ca, cb, _, _ = coords[step]
        here = pl.ds(k * size, size)
        first, second, _, _ = hits[step]
        scatter_first(step, 1, k).wait_recv()
        scatter_second(step, k).wait_recv()
        mine = jnp.where(
            second,
            jnp.where(first, a_ref[at((ca * 2 + cb) * piece, k)], r1_ref[step, 1, here]),
            r2_ref[step, here],
        )
        zout_ref[0, step, here] = mine
        zout_ref[1, step, here] = mine
        own = at((ca * 2 + cb) * piece, k)
        w_ref[step, own] = mine

    def stream(k, step, up):
        ca, cb, _, _ = coords[step]
        here = pl.ds(k * size, size)
        own = at((ca * 2 + cb) * piece, k)
        _, _, level, below = hits[step]
        side = 0 if up else 1
        source = below if up else jnp.logical_not(jnp.logical_or(level, below))

        @pl.when(has_left if up else has_right)
        def _():
            along(step, k, up).wait_recv()
            got = zin_ref[side, step, here]
            zout_ref[side, step, here] = jnp.where(level, zout_ref[side, step, here], got)
            w_ref[step, own] = jnp.where(source, got, w_ref[step, own])

        @pl.when(has_right if up else has_left)
        def _():
            along(step, k, up).start()

    def both_ways(near, far):
        @pl.when(cz < line // 2)
        def _():
            if near is not None:
                stream(*near, True)
            if far is not None:
                stream(*far, False)

        @pl.when(cz >= line // 2)
        def _():
            if near is not None:
                stream(*near, False)
            if far is not None:
                stream(*far, True)

    count = len(pairs)
    for tick in range(count + LAG):
        near = far = None
        if tick < count:
            near = pairs[tick]
            ready(*near)
        if tick >= LAG:
            far = pairs[tick - LAG]
        both_ways(near, far)
        if far is not None:
            gather(far[1], far[0], 5).start()
            gather(far[1], far[0], 6).start()

    for k, step in pairs:
        gather(step, k, 5).wait_recv()
        gather(step, k, 7).start()

    for k, step in pairs:
        gather(step, k, 6).wait_recv()
        gather(step, k, 7).wait_recv()

    half = chans // 2
    keep = day * half
    give = (1 - day) * half
    lanes = lax.broadcasted_iota(jnp.int32, (chans, a_ref.shape[1]), 1)
    low = jnp.where(lanes < a_ref.shape[1] // 2, 1.0, 0.0).astype(jnp.bfloat16)
    high = jnp.where(lanes < a_ref.shape[1] // 2, 0.0, 1.0).astype(jnp.bfloat16)

    def cross(g, carry):
        base = pl.multiple_of(g * chans, 16)
        kept = pl.ds(pl.multiple_of(base + keep, 16), half)
        given = pl.ds(pl.multiple_of(base + give, 16), half)
        left = jnp.concatenate([a_ref[kept], b_ref[kept], a_ref[given], b_ref[given]], axis=0)
        blocks = []
        for step in range(STEPS):
            block = w_ref[step, pl.ds(base, chans)]
            blocks += [block * low, block * high]
        right = jnp.concatenate(blocks, axis=0)
        out = lax.dot_general(
            left, right, (((1,), (1,)), ((), ())), preferred_element_type=jnp.float32
        )
        spot = pl.ds(pl.multiple_of(g * chans, 16), chans)
        o_ref[spot] = out[:chans].astype(jnp.bfloat16)
        c_send[spot] = out[chans:].astype(jnp.bfloat16)
        return carry

    parts = day_send.shape[0]
    per = groups // parts

    def swap(part):
        where = pl.ds(part * per * chans, per * chans)
        return pltpu.make_async_remote_copy(
            src_ref=c_send.at[where], dst_ref=c_recv.at[where],
            send_sem=day_send.at[part], recv_sem=day_recv.at[part],
            device_id={"day": 1 - day}, device_id_type=MESH_ID,
        )

    for part in range(parts):
        lax.fori_loop(part * per, (part + 1) * per, cross, 0, unroll=5)
        swap(part).start()

    for part in range(parts):
        where = pl.ds(part * per * chans, per * chans)
        swap(part).wait_recv()
        total = o_ref[where].astype(jnp.float32) + c_recv[where].astype(jnp.float32)
        o_ref[where] = total.astype(jnp.bfloat16)

    for part in range(parts):
        swap(part).wait_send()
    for k, step in pairs:
        for part in range(2):
            scatter_first(step, part, k).wait_send()
        scatter_second(step, k).wait_send()
        for phase in (5, 6, 7):
            gather(step, k, phase).wait_send()

    @pl.when(has_right)
    def _():
        for k, step in pairs:
            along(step, k, True).wait_send()

    @pl.when(has_left)
    def _():
        for k, step in pairs:
            along(step, k, False).wait_send()


def local(spectra, owners):
    chans, windows, width = spectra.shape
    bins = width // 2
    groups = bins // 2
    line = lax.axis_size("chan") // 4
    windows_all = windows * lax.axis_size("day")
    re_part, im_part = whiten(spectra, bins)

    plain = jnp.concatenate(
        [re_part[..., :groups], im_part[..., :groups], re_part[..., groups:], im_part[..., groups:]],
        axis=1,
    )
    plain = lax.optimization_barrier(plain)
    plain = plain.transpose(2, 0, 1).reshape(groups * chans, 4 * windows)
    rows, lanes = plain.shape
    piece = rows // 4
    chunks = chunks_of(piece)
    bf16 = jnp.bfloat16
    vmem = pl.BlockSpec(memory_space=pltpu.VMEM)
    summed = pl.pallas_call(
        functools.partial(kernel, line, chunks, chans, groups),
        out_shape=jax.ShapeDtypeStruct((groups * chans, 4 * chans), bf16),
        in_specs=[pl.BlockSpec(memory_space=pltpu.SMEM), vmem],
        out_specs=vmem,
        scratch_shapes=[
            pltpu.VMEM((rows, lanes), bf16),
            pltpu.VMEM((STEPS, rows, lanes), bf16),
            pltpu.VMEM((STEPS, 2, piece, lanes), bf16),
            pltpu.VMEM((STEPS, piece, lanes), bf16),
            pltpu.VMEM((STEPS, piece, lanes), bf16),
            pltpu.VMEM((2, STEPS, piece, lanes), bf16),
            pltpu.VMEM((2, STEPS, piece, lanes), bf16),
            pltpu.VMEM((groups * chans, 4 * chans), bf16),
            pltpu.VMEM((groups * chans, 4 * chans), bf16),
            pltpu.SemaphoreType.DMA((STEPS, 8, chunks)),
            pltpu.SemaphoreType.DMA((STEPS, 8, chunks)),
            pltpu.SemaphoreType.DMA((4,)),
            pltpu.SemaphoreType.DMA((4,)),
        ],
        compiler_params=pltpu.CompilerParams(collective_id=0, has_side_effects=True),
    )(owners, plain)

    norm = 1.0 / math.sqrt(windows_all * bins)
    table = jnp.asarray(lag_table(bins, LAGS))
    half = chans // 2
    turned = summed.reshape(groups, chans, 4 * chans).transpose(1, 2, 0)
    turned = lax.optimization_barrier(turned).reshape(2, half, STEPS, 2, chans, groups)
    full = jnp.concatenate(
        [turned[part, :, :, which] for part in range(2) for which in range(2)], axis=-1
    )
    full = full.transpose(1, 0, 2, 3).reshape(STEPS * half * chans, 2 * bins)
    full = lax.optimization_barrier(full)
    lagged = jnp.dot(full, table, preferred_element_type=jnp.float32) * norm
    lagged = lagged.reshape(STEPS, half, chans, LAGS)
    return lagged.astype(bf16)


def solution(mesh):
    placed = (P("chan", "day", None), P())
    return jax.shard_map(
        local,
        mesh=mesh,
        in_specs=placed,
        out_specs=P(None, ("chan", "day"), None, None),
        check_vma=False,
    )
```
